32 devices in a mesh: tile: 4 (over x, core), frame: 8 (over z, y).
Axes of the slice: x: 2, y: 2, z: 4, core: 2. Of those that a mesh axis runs over, the one named last changes fastest.
Arguments:
- queries: bfloat16 [8192, 1536], P(('tile', 'frame')), may hold values from -5 to 5
- keys: bfloat16 [8192, 1536], P(('tile', 'frame')), may hold values from -5 to 5
- values: bfloat16 [8192, 1536], P(('tile', 'frame')), may hold values from -6 to 6
- block_lists: int32 [64, 26], replicated, may hold values from -1 to 63, as said below
Outputs:
- attended: bfloat16 [8192, 1536], P(('tile', 'frame'))
The draws below stay inside these ranges and needn't reach their ends.
Inputs may be any that keep to these rules, and one draw needn't show every extreme that they name: `block_lists`: block b belongs to spatial tile (b // 2) // 8 and frame group (b // 2) % 8. Row b lists first, without repeats, the key blocks that query block b attends to, then -1 to its end. Every listed block lies at a squared distance of at most 4 from block b in (tile, frame group), and all blocks of b's own tile and frame group are listed.
All inputs are finite; a program needn't handle non-finite values.
Results may differ from the reference program's by a relative error of at most 0.004.
Values may be sent and summed in bfloat16 or wider, within the bound.
A program may use at most 128 MiB of HBM per device.

```python
import math
import jax
import jax.numpy as jnp
from jax import lax

HEADS = 12
DH = 128
BLK = 128
BLK_DEV = 2
WIDTH = 1536
TILES = 4
GROUPS = 8
TOKENS = 8192
QBLOCKS = 64
LIST = 26


def offset_pairs():
    return [(across, along) for across in range(-2, 3) for along in range(-2, 3) if across * across + along * along <= 4]


def draw_block_lists(key, part):
    pairs = offset_pairs()
    tile_off = jnp.array([entry[0] for entry in pairs], jnp.int32)
    group_off = jnp.array([entry[1] for entry in pairs], jnp.int32)
    reach_sq = tile_off * tile_off + group_off * group_off
    blocks = jnp.arange(QBLOCKS, dtype=jnp.int32)
    device = blocks // BLK_DEV
    tile_of = device // GROUPS
    group_of = device % GROUPS
    radius = jax.random.randint(key, (QBLOCKS,), 1, 4)
    centre = (TILES // 2 * GROUPS + GROUPS // 2) * BLK_DEV
    radius = jnp.where(blocks == centre, 3, radius)
    limit_sq = jnp.where(radius == 3, 4, radius)
    tile_key = tile_of[:, None] + tile_off[None, :]
    group_key = group_of[:, None] + group_off[None, :]
    usable = (reach_sq[None, :] <= limit_sq[:, None]) & (tile_key >= 0) & (tile_key < TILES) & (group_key >= 0) & (group_key < GROUPS)
    base_block = (tile_key * GROUPS + group_key) * BLK_DEV
    within = jnp.arange(BLK_DEV, dtype=jnp.int32)
    block_ids = (base_block[:, :, None] + within[None, None, :]).reshape(QBLOCKS, LIST)
    usable = jnp.broadcast_to(usable[:, :, None], (QBLOCKS, len(pairs), BLK_DEV)).reshape(QBLOCKS, LIST)
    ordering_key = jnp.where(usable, 0, LIST) + jnp.arange(LIST, dtype=jnp.int32)[None, :]
    permuted = jnp.argsort(ordering_key, axis=1)
    block_ids = jnp.take_along_axis(block_ids, permuted, axis=1)
    usable = jnp.take_along_axis(usable, permuted, axis=1)
    return jnp.where(usable, block_ids, -1).astype(jnp.int32)


def base_field(key, scale, salt):
    noise_key = jax.random.fold_in(key, salt)
    field = jax.random.normal(noise_key, (TOKENS, WIDTH), jnp.float32) * scale
    return jnp.clip(field, -5.0, 5.0)


def draw_queries(key, part):
    field = base_field(key, 1.3, 1)
    return field.astype(jnp.bfloat16)


def draw_keys(key, part):
    field = base_field(key, 1.3, 2)
    return field.astype(jnp.bfloat16)


def draw_values(key, part):
    offsets = jax.random.normal(jax.random.fold_in(key, 4), (QBLOCKS, WIDTH), jnp.float32)
    noise = jax.random.normal(jax.random.fold_in(key, 3), (TOKENS, WIDTH), jnp.float32)
    field = noise + jnp.repeat(offsets, BLK, axis=0)
    return jnp.clip(field, -6.0, 6.0).astype(jnp.bfloat16)


def setup_inputs(seed: int = 0) -> dict:
    streams_of = jax.random.split(jax.random.key(seed), 5)
    queries = draw_queries(jax.random.fold_in(streams_of[4], 71), 0)
    keys = draw_keys(jax.random.fold_in(streams_of[4], 71), 0)
    values = draw_values(jax.random.fold_in(streams_of[4], 71), 0)
    block_lists = draw_block_lists(jax.random.fold_in(streams_of[4], 71), 0)
    return dict(queries=queries, keys=keys, values=values, block_lists=block_lists)


def reference(queries, keys, values, block_lists):
    query_blocks = queries.reshape(QBLOCKS, BLK, HEADS, DH)
    key_blocks = keys.reshape(QBLOCKS, BLK, HEADS, DH)
    value_blocks = values.reshape(QBLOCKS, BLK, HEADS, DH)
    scale = 1.0 / math.sqrt(DH)

    def one_block(inputs):
        query_rows, listed = inputs
        listed_ok = listed >= 0
        picked = jnp.where(listed_ok, listed, 0).astype(jnp.int32)
        key_rows = key_blocks[picked].reshape(LIST * BLK, HEADS, DH)
        value_rows = value_blocks[picked].reshape(LIST * BLK, HEADS, DH)
        allowed = jnp.repeat(listed_ok, BLK)
        scores = jnp.einsum('qhd,khd->hqk', query_rows.astype(jnp.float32), key_rows.astype(jnp.float32)) * scale
        masked = jnp.where(allowed[None, None, :], scores, -1e+30)
        top = lax.optimization_barrier(jnp.max(masked, axis=2, keepdims=True))
        weights = jnp.where(allowed[None, None, :], jnp.exp(masked - top), 0.0)
        denom = lax.optimization_barrier(jnp.sum(weights, axis=2))
        rounded = lax.optimization_barrier(weights.astype(jnp.bfloat16)).astype(jnp.float32)
        mixed = jnp.einsum('hqk,khd->qhd', rounded, value_rows.astype(jnp.float32))
        result = mixed / denom.T[:, :, None]
        return result.reshape(BLK, HEADS * DH).astype(jnp.bfloat16)
    outputs = lax.map(one_block, (query_blocks, block_lists))
    return outputs.reshape(QBLOCKS * BLK, HEADS * DH)
```

```python
import math

import jax
import jax.numpy as jnp
from jax import lax
from jax.experimental import pallas as pl
from jax.experimental.pallas import tpu as pltpu
from jax.sharding import PartitionSpec as P

HEADS = 12
DH = 128
BLK = 128
PER = 2
CHUNKS = HEADS // PER
HALF = PER * DH
NEGATIVE = -1e30
FLOOR = -1e29
SCALE = math.log2(math.e) / math.sqrt(DH)

SELF, PART, X1, X2, X3, ZA, ZB, PZB, XZB = range(9)
SLOTS = 9
OWN = (SELF, PART, X1, X2, X3, ZA, ZB)
GUEST = (SELF, PART, X1, ZB, PZB, XZB)
BIAS_ROW = {(0, slot): 2 * n for n, slot in enumerate(OWN)}
BIAS_ROW.update({(1, slot): 2 * (len(OWN) + n) for n, slot in enumerate(GUEST)})
BIAS_ROWS = 32
AHEAD = 1
LAG_X = 2
LAG_OUT = 4
VIA_X = tuple(range(0, CHUNKS, 2))
VIA_Z = tuple(range(1, CHUNKS, 2))


def geometry():
    tiles, groups = lax.axis_size("tile"), lax.axis_size("frame")
    t, g = lax.axis_index("tile"), lax.axis_index("frame")
    f = 2 * lax.rem(t, 2) - 1
    d = 2 * lax.rem(g, 2) - 1
    offsets = (
        (0, 0), (-f, 0), (f, 0), (2 * f, 0), (-2 * f, 0), (0, 2 * d), (0, -2 * d), (-f, -2 * d), (f, -2 * d),
    )
    return tiles, groups, t, g, f, d, offsets


def kernel(
    q_hbm, k_hbm, v_hbm, lists_ref, o_ref,
    qbuf, bias, buf, acc, top, total, guest_out, guest_stat, back_out, back_stat,
    own_sem, send_sem, recv_sem, q_send, q_recv, out_send, out_recv, stat_send, stat_recv,
):
    tiles, groups, t, g, f, d, offsets = geometry()

    def inside(dt, dg):
        a, b = t + dt, g + dg
        return (a >= 0) & (a < tiles) & (b >= 0) & (b < groups)

    valid = [inside(*offset) for offset in offsets]
    peers = ((-f, 0), (0, -d), (0, 2), (0, -2), (f, 0), (2, 0), (-2, 0))

    def own_copy(j, which):
        ref = (k_hbm, v_hbm, q_hbm)[which]
        place = qbuf.at[0, j] if which == 2 else buf.at[SELF, j, :, pl.ds(which * HALF, HALF)]
        return pltpu.make_async_copy(ref.at[:, pl.ds(j * HALF, HALF)], place, own_sem.at[j, which])

    for j in range(CHUNKS):
        for which in range(3):
            own_copy(j, which).start()

    barrier = pltpu.get_barrier_semaphore()
    for dt, dg in peers:
        @pl.when(inside(dt, dg))
        def _():
            pl.semaphore_signal(
                barrier, inc=1, device_id=(t + dt, g + dg), device_id_type=pl.DeviceIdType.MESH
            )
    pl.semaphore_wait(barrier, sum(inside(*peer).astype(jnp.int32) for peer in peers))

    every = tuple(range(CHUNKS))
    moves = (
        (SELF, X1, (f, 0), every),
        (SELF, ZB, (0, 2 * d), every),
        (SELF, PART, (-f, 0), every),
        (SELF, X2, (-2 * f, 0), every),
        (SELF, ZA, (0, -2 * d), every),
        (X1, X3, (-f, 0), every),
        (X1, XZB, (0, 2 * d), VIA_Z),
        (ZB, PZB, (-f, 0), every),
        (ZB, XZB, (f, 0), VIA_X),
    )

    def among(j, chunks):
        hit = j == chunks[0]
        for other in chunks[1:]:
            hit = hit | (j == other)
        return hit

    def each_move(j, sources, act):
        for index, (source, slot, place, chunks) in enumerate(moves):
            if source not in sources or not chunks:
                continue
            where = inside(*place) & valid[source]
            if len(chunks) < CHUNKS:
                where = where & among(j, chunks)

            @pl.when(where)
            def _():
                act(
                    pltpu.make_async_remote_copy(
                        src_ref=buf.at[source, j],
                        dst_ref=buf.at[slot, j],
                        send_sem=send_sem.at[index, j],
                        recv_sem=recv_sem.at[slot, j],
                        device_id=(t + place[0], g + place[1]),
                        device_id_type=pl.DeviceIdType.MESH,
                    )
                )

    def to_pair(src, dst, send, recv):
        return pltpu.make_async_remote_copy(
            src_ref=src, dst_ref=dst, send_sem=send, recv_sem=recv,
            device_id=(t, g - d), device_id_type=pl.DeviceIdType.MESH,
        )

    def q_move(j):
        return to_pair(qbuf.at[0, j], qbuf.at[1, j], q_send.at[j], q_recv.at[j])

    def out_move(j):
        return to_pair(guest_out.at[j], back_out.at[j], out_send.at[j], out_recv.at[j])

    def stat_move(j):
        return to_pair(guest_stat.at[j], back_stat.at[j], stat_send.at[j], stat_recv.at[j])

    def arrived(slot, j):
        pltpu.make_async_copy(buf.at[slot, j], buf.at[slot, j], recv_sem.at[slot, j]).wait()

    def mask_rows():
        lists = lists_ref[...]
        block = lax.broadcasted_iota(jnp.int32, lists.shape, 1)
        first = lax.broadcasted_iota(jnp.int32, (lists.shape[0], 2 * BLK), 1) < BLK
        for who, slots, base in ((0, OWN, 2 * (t * groups + g)), (1, GUEST, 2 * (t * groups + g - d))):
            upper = jnp.sum(jnp.where(block == base, lists, 0), axis=1, keepdims=True)
            lower = jnp.sum(jnp.where(block == base + 1, lists, 0), axis=1, keepdims=True)
            listed = jnp.where(first, upper, lower)
            for slot in slots:
                dt, dg = offsets[slot]
                for half in range(2):
                    name = 2 * ((t + dt) * groups + g + dg) + half
                    hit = jnp.max(jnp.where(listed == name, 1, 0), axis=0, keepdims=True)
                    row = BIAS_ROW[who, slot] + half
                    bias[row:row + 1, :] = jnp.where(hit > 0, 0.0, NEGATIVE)

    def compute(slot, j, users):
        for hh in range(PER):
            k = buf[slot, j, :, hh * DH:(hh + 1) * DH]
            v = buf[slot, j, :, HALF + hh * DH:HALF + (hh + 1) * DH]
            head = j * PER + hh
            for who in users:
                row = BIAS_ROW[who, slot]
                b0, b1 = bias[row:row + 1, :], bias[row + 1:row + 2, :]
                s = lax.dot_general(
                    k, qbuf[who, j, :, hh * DH:(hh + 1) * DH], (((1,), (1,)), ((), ())),
                    preferred_element_type=jnp.float32,
                )
                s0, s1 = s[:BLK], s[BLK:]
                peak = jnp.maximum(
                    jnp.max(s0, axis=0, keepdims=True) * SCALE + b0,
                    jnp.max(s1, axis=0, keepdims=True) * SCALE + b1,
                )
                if slot == SELF:
                    new = jnp.maximum(peak, FLOOR)
                else:
                    old = top[who, head, 0:1, :]
                    new = jnp.maximum(old, peak)
                p = jnp.concatenate(
                    [jnp.exp2(s0 * SCALE - (new - b0)), jnp.exp2(s1 * SCALE - (new - b1))], axis=0
                )
                part = jnp.sum(p.reshape(2 * BLK // 8, 8, 2 * BLK), axis=0)
                mixed = lax.dot_general(
                    v, p.astype(jnp.bfloat16), (((0,), (0,)), ((), ())), preferred_element_type=jnp.float32
                )
                if slot != SELF:
                    rescale = jnp.exp2(old - new)
                    part = part + total[who, head] * rescale
                    mixed = mixed + acc[who, head] * rescale
                top[who, head, 0:1, :] = new
                total[who, head] = part
                acc[who, head] = mixed

    def pack_guest(j):
        for hh in range(PER):
            head = j * PER + hh
            guest_out[j, hh * DH:(hh + 1) * DH, :] = acc[1, head].astype(jnp.bfloat16)
            guest_stat[j, 2 * hh:2 * hh + 1, :] = top[1, head, 0:1, :]
            guest_stat[j, 2 * hh + 1:2 * hh + 2, :] = jnp.sum(total[1, head], axis=0, keepdims=True)

    def finish(j):
        for hh in range(PER):
            head = j * PER + hh
            m1, m2 = top[0, head, 0:1, :], back_stat[j, 2 * hh:2 * hh + 1, :]
            m = jnp.maximum(m1, m2)
            e1, e2 = jnp.exp2(m1 - m), jnp.exp2(m2 - m)
            l1 = jnp.sum(total[0, head], axis=0, keepdims=True)
            denom = l1 * e1 + back_stat[j, 2 * hh + 1:2 * hh + 2, :] * e2
            other = back_out[j, hh * DH:(hh + 1) * DH, :].astype(jnp.float32)
            mixed = acc[0, head] * (e1 / denom) + other * (e2 / denom)
            cols = pl.ds(pl.multiple_of(head * DH, DH), DH)
            o_ref[:, cols] = mixed.T.astype(jnp.bfloat16)

    def launch(j):
        own_copy(j, 0).wait()
        own_copy(j, 1).wait()
        each_move(j, (SELF,), lambda copy: copy.start())

    def when_valid(slot, j, users, wait=True):
        @pl.when(valid[slot])
        def _():
            if wait:
                arrived(slot, j)
            compute(slot, j, users)

    for j in range(AHEAD):
        launch(j)

    def send_q(j, carry):
        own_copy(j, 2).wait()
        q_move(j).start()
        return carry
    lax.fori_loop(0, CHUNKS, send_q, 0)
    mask_rows()

    def step(tick, carry):
        @pl.when(tick + AHEAD < CHUNKS)
        def _():
            launch(tick + AHEAD)

        @pl.when(tick < CHUNKS)
        def _():
            compute(SELF, tick, (0,))
            q_move(tick).wait_recv()
            compute(SELF, tick, (1,))
            when_valid(PART, tick, (0, 1))
            for slot in (X1, ZB):
                @pl.when(valid[slot])
                def _():
                    arrived(slot, tick)
                each_move(tick, (slot,), lambda copy: copy.start())
            for slot in (X1, ZB):
                when_valid(slot, tick, (0, 1), wait=False)

        j = tick - LAG_X

        @pl.when((j >= 0) & (j < CHUNKS))
        def _():
            when_valid(PZB, j, (1,))
            when_valid(XZB, j, (1,))
            pack_guest(j)

        @pl.when(tick < CHUNKS)
        def _():
            when_valid(X2, tick, (0,))
            when_valid(ZA, tick, (0,))

        @pl.when((j >= 0) & (j < CHUNKS))
        def _():
            when_valid(X3, j, (0,))
            out_move(j).start()
            stat_move(j).start()

        last = tick - LAG_OUT

        @pl.when((last >= 0) & (last < CHUNKS))
        def _():
            out_move(last).wait_recv()
            stat_move(last).wait_recv()
            finish(last)
        return carry
    lax.fori_loop(0, CHUNKS + LAG_OUT, step, 0)

    def drain(j, carry):
        each_move(j, tuple(range(SLOTS)), lambda copy: copy.wait_send())
        q_move(j).wait_send()
        out_move(j).wait_send()
        stat_move(j).wait_send()
        return carry
    lax.fori_loop(0, CHUNKS, drain, 0)


def shards(queries, keys, values, block_lists):
    rows, width = queries.shape
    vmem = pl.BlockSpec(memory_space=pltpu.VMEM)
    anywhere = pl.BlockSpec(memory_space=pl.ANY)
    return pl.pallas_call(
        kernel,
        out_shape=jax.ShapeDtypeStruct((rows, width), jnp.bfloat16),
        in_specs=[anywhere, anywhere, anywhere, vmem],
        out_specs=vmem,
        scratch_shapes=[
            pltpu.VMEM((2, CHUNKS, rows, HALF), jnp.bfloat16),
            pltpu.VMEM((BIAS_ROWS, rows), jnp.float32),
            pltpu.VMEM((SLOTS, CHUNKS, rows, 2 * HALF), jnp.bfloat16),
            pltpu.VMEM((2, HEADS, DH, rows), jnp.float32),
            pltpu.VMEM((2, HEADS, 8, rows), jnp.float32),
            pltpu.VMEM((2, HEADS, 8, rows), jnp.float32),
            pltpu.VMEM((CHUNKS, HALF, rows), jnp.bfloat16),
            pltpu.VMEM((CHUNKS, 8, rows), jnp.float32),
            pltpu.VMEM((CHUNKS, HALF, rows), jnp.bfloat16),
            pltpu.VMEM((CHUNKS, 8, rows), jnp.float32),
            pltpu.SemaphoreType.DMA((CHUNKS, 3)),
            pltpu.SemaphoreType.DMA((9, CHUNKS)),
            pltpu.SemaphoreType.DMA((SLOTS, CHUNKS)),
            pltpu.SemaphoreType.DMA((CHUNKS,)),
            pltpu.SemaphoreType.DMA((CHUNKS,)),
            pltpu.SemaphoreType.DMA((CHUNKS,)),
            pltpu.SemaphoreType.DMA((CHUNKS,)),
            pltpu.SemaphoreType.DMA((CHUNKS,)),
            pltpu.SemaphoreType.DMA((CHUNKS,)),
        ],
        compiler_params=pltpu.CompilerParams(
            collective_id=0, has_side_effects=True, vmem_limit_bytes=67043328
        ),
    )(queries, keys, values, block_lists.T)


def solution(mesh):
    placed = P(("tile", "frame"), None)
    return jax.shard_map(
        shards, mesh=mesh, in_specs=(placed, placed, placed, P()), out_specs=placed, check_vma=False
    )
```

```python
import math

import jax
import jax.numpy as jnp
from jax import lax
from jax.experimental import pallas as pl
from jax.experimental.pallas import tpu as pltpu
from jax.sharding import PartitionSpec as P

HEADS = 12
DH = 128
BLK = 128
PER = 2
CHUNKS = HEADS // PER
HALF = PER * DH
NEGATIVE = -1e30
SCALE = math.log2(math.e) / math.sqrt(DH)

SELF, PART, X1, X2, X3, ZA, ZB, PZB, XZB = range(9)
SLOTS = 9
OWN = (SELF, PART, X1, X2, X3, ZA, ZB)
GUEST = (SELF, PART, X1, ZB, PZB, XZB)
BIAS_ROW = {(0, slot): 2 * n for n, slot in enumerate(OWN)}
BIAS_ROW.update({(1, slot): 2 * (len(OWN) + n) for n, slot in enumerate(GUEST)})
BIAS_ROWS = 32
AHEAD = 1
LAG_X = 2
LAG_OUT = 4
VIA_X = tuple(range(0, CHUNKS, 2))
VIA_Z = tuple(range(1, CHUNKS, 2))


def geometry():
    tiles, groups = lax.axis_size("tile"), lax.axis_size("frame")
    t, g = lax.axis_index("tile"), lax.axis_index("frame")
    f = 2 * lax.rem(t, 2) - 1
    d = 2 * lax.rem(g, 2) - 1
    offsets = (
        (0, 0), (-f, 0), (f, 0), (2 * f, 0), (-2 * f, 0), (0, 2 * d), (0, -2 * d), (-f, -2 * d), (f, -2 * d),
    )
    return tiles, groups, t, g, f, d, offsets


def kernel(
    q_hbm, k_hbm, v_hbm, lists_ref, o_ref,
    qbuf, bias, buf, acc, top, total, guest_out, guest_stat, back_out, back_stat,
    own_sem, send_sem, recv_sem, q_send, q_recv, out_send, out_recv, stat_send, stat_recv,
):
    tiles, groups, t, g, f, d, offsets = geometry()

    def inside(dt, dg):
        a, b = t + dt, g + dg
        return (a >= 0) & (a < tiles) & (b >= 0) & (b < groups)

    valid = [inside(*offset) for offset in offsets]
    peers = ((-f, 0), (0, -d), (0, 2), (0, -2), (f, 0), (2, 0), (-2, 0))

    def own_copy(j, which):
        ref = (k_hbm, v_hbm, q_hbm)[which]
        place = qbuf.at[0, j] if which == 2 else buf.at[SELF, j, :, pl.ds(which * HALF, HALF)]
        return pltpu.make_async_copy(ref.at[:, pl.ds(j * HALF, HALF)], place, own_sem.at[j, which])

    for j in range(CHUNKS):
        for which in range(3):
            own_copy(j, which).start()

    barrier = pltpu.get_barrier_semaphore()
    for dt, dg in peers:
        @pl.when(inside(dt, dg))
        def _():
            pl.semaphore_signal(
                barrier, inc=1, device_id=(t + dt, g + dg), device_id_type=pl.DeviceIdType.MESH
            )
    pl.semaphore_wait(barrier, sum(inside(*peer).astype(jnp.int32) for peer in peers))

    every = tuple(range(CHUNKS))
    moves = (
        (SELF, X1, (f, 0), every),
        (SELF, ZB, (0, 2 * d), every),
        (SELF, PART, (-f, 0), every),
        (SELF, X2, (-2 * f, 0), every),
        (SELF, ZA, (0, -2 * d), every),
        (X1, X3, (-f, 0), every),
        (X1, XZB, (0, 2 * d), VIA_Z),
        (ZB, PZB, (-f, 0), every),
        (ZB, XZB, (f, 0), VIA_X),
    )

    def among(j, chunks):
        hit = j == chunks[0]
        for other in chunks[1:]:
            hit = hit | (j == other)
        return hit

    def each_move(j, sources, act):
        for index, (source, slot, place, chunks) in enumerate(moves):
            if source not in sources or not chunks:
                continue
            where = inside(*place) & valid[source]
            if len(chunks) < CHUNKS:
                where = where & among(j, chunks)

            @pl.when(where)
            def _():
                act(
                    pltpu.make_async_remote_copy(
                        src_ref=buf.at[source, j],
                        dst_ref=buf.at[slot, j],
                        send_sem=send_sem.at[index, j],
                        recv_sem=recv_sem.at[slot, j],
                        device_id=(t + place[0], g + place[1]),
                        device_id_type=pl.DeviceIdType.MESH,
                    )
                )

    def to_pair(src, dst, send, recv):
        return pltpu.make_async_remote_copy(
            src_ref=src, dst_ref=dst, send_sem=send, recv_sem=recv,
            device_id=(t, g - d), device_id_type=pl.DeviceIdType.MESH,
        )

    def q_move(j):
        return to_pair(qbuf.at[0, j], qbuf.at[1, j], q_send.at[j], q_recv.at[j])

    def out_move(j):
        return to_pair(guest_out.at[j], back_out.at[j], out_send.at[j], out_recv.at[j])

    def stat_move(j):
        return to_pair(guest_stat.at[j], back_stat.at[j], stat_send.at[j], stat_recv.at[j])

    def arrived(slot, j):
        pltpu.make_async_copy(buf.at[slot, j], buf.at[slot, j], recv_sem.at[slot, j]).wait()

    def mask_rows():
        lists = lists_ref[...]
        block = lax.broadcasted_iota(jnp.int32, lists.shape, 1)
        second = lax.broadcasted_iota(jnp.int32, (1, 2 * BLK), 1) // BLK
        for who, slots, base in ((0, OWN, 2 * (t * groups + g)), (1, GUEST, 2 * (t * groups + g - d))):
            for half in range(2):
                listed = jnp.sum(jnp.where(block == base + half, lists, 0), axis=1, keepdims=True)
                for slot in slots:
                    dt, dg = offsets[slot]
                    names = 2 * ((t + dt) * groups + g + dg) + second
                    hit = jnp.max(jnp.where(listed == names, 1, 0), axis=0, keepdims=True)
                    row = BIAS_ROW[who, slot] + half
                    bias[row:row + 1, :] = jnp.where(hit > 0, 0.0, NEGATIVE)

    def compute(slot, j, users):
        for hh in range(PER):
            k = buf[slot, j, :, hh * DH:(hh + 1) * DH]
            v = buf[slot, j, :, HALF + hh * DH:HALF + (hh + 1) * DH]
            head = j * PER + hh
            for who in users:
                row = BIAS_ROW[who, slot]
                s = lax.dot_general(
                    qbuf[who, j, :, hh * DH:(hh + 1) * DH], k, (((1,), (1,)), ((), ())),
                    preferred_element_type=jnp.float32,
                )
                s = jnp.concatenate(
                    [s[:BLK] * SCALE + bias[row:row + 1, :], s[BLK:] * SCALE + bias[row + 1:row + 2, :]], axis=0
                )
                peak = jnp.max(s, axis=1, keepdims=True)
                if slot == SELF:
                    new = jnp.broadcast_to(peak, (2 * BLK, DH))
                else:
                    old = top[who, head]
                    new = jnp.maximum(old, peak)
                p = jnp.exp2(s - jnp.concatenate([new, new], axis=1))
                part = p[:, :DH] + p[:, DH:]
                mixed = jnp.dot(p.astype(jnp.bfloat16), v, preferred_element_type=jnp.float32)
                if slot != SELF:
                    rescale = jnp.exp2(old - new)
                    part = part + total[who, head] * rescale
                    mixed = mixed + acc[who, head] * rescale
                top[who, head] = new
                total[who, head] = part
                acc[who, head] = mixed

    def pack_guest(j):
        lane = lax.broadcasted_iota(jnp.int32, (2 * BLK, DH), 1)
        table = jnp.zeros((2 * BLK, DH), jnp.float32)
        for hh in range(PER):
            head = j * PER + hh
            guest_out[j, :, hh * DH:(hh + 1) * DH] = acc[1, head].astype(jnp.bfloat16)
            denom = jnp.sum(total[1, head], axis=1, keepdims=True)
            table = jnp.where(lane == 2 * hh, top[1, head], table)
            table = jnp.where(lane == 2 * hh + 1, denom, table)
        guest_stat[j] = table.T[:8]

    def finish(j):
        table = jnp.concatenate([back_stat[j]] * (DH // 8), axis=0).T
        for hh in range(PER):
            head = j * PER + hh
            m1, m2 = top[0, head], table[:, 2 * hh:2 * hh + 1]
            m = jnp.maximum(m1, m2)
            e1, e2 = jnp.exp2(m1 - m), jnp.exp2(m2 - m)
            l1 = jnp.sum(total[0, head], axis=1, keepdims=True)
            denom = l1 * e1 + table[:, 2 * hh + 1:2 * hh + 2] * e2
            other = back_out[j, :, hh * DH:(hh + 1) * DH].astype(jnp.float32)
            cols = pl.ds(pl.multiple_of(head * DH, DH), DH)
            o_ref[:, cols] = ((acc[0, head] * e1 + other * e2) / denom).astype(jnp.bfloat16)

    def launch(j):
        own_copy(j, 0).wait()
        own_copy(j, 1).wait()
        each_move(j, (SELF,), lambda copy: copy.start())

    def when_valid(slot, j, users, wait=True):
        @pl.when(valid[slot])
        def _():
            if wait:
                arrived(slot, j)
            compute(slot, j, users)

    for j in range(AHEAD):
        launch(j)

    def send_q(j, carry):
        own_copy(j, 2).wait()
        q_move(j).start()
        return carry
    lax.fori_loop(0, CHUNKS, send_q, 0)
    mask_rows()

    def step(tick, carry):
        @pl.when(tick + AHEAD < CHUNKS)
        def _():
            launch(tick + AHEAD)

        @pl.when(tick < CHUNKS)
        def _():
            compute(SELF, tick, (0,))
            q_move(tick).wait_recv()
            compute(SELF, tick, (1,))
            when_valid(PART, tick, (0, 1))
            for slot in (X1, ZB):
                @pl.when(valid[slot])
                def _():
                    arrived(slot, tick)
                each_move(tick, (slot,), lambda copy: copy.start())
            for slot in (X1, ZB):
                when_valid(slot, tick, (0, 1), wait=False)

        j = tick - LAG_X

        @pl.when((j >= 0) & (j < CHUNKS))
        def _():
            when_valid(PZB, j, (1,))
            when_valid(XZB, j, (1,))
            pack_guest(j)

        @pl.when(tick < CHUNKS)
        def _():
            when_valid(X2, tick, (0,))
            when_valid(ZA, tick, (0,))

        @pl.when((j >= 0) & (j < CHUNKS))
        def _():
            when_valid(X3, j, (0,))
            out_move(j).start()
            stat_move(j).start()

        last = tick - LAG_OUT

        @pl.when((last >= 0) & (last < CHUNKS))
        def _():
            out_move(last).wait_recv()
            stat_move(last).wait_recv()
            finish(last)
        return carry
    lax.fori_loop(0, CHUNKS + LAG_OUT, step, 0)

    def drain(j, carry):
        each_move(j, tuple(range(SLOTS)), lambda copy: copy.wait_send())
        q_move(j).wait_send()
        out_move(j).wait_send()
        stat_move(j).wait_send()
        return carry
    lax.fori_loop(0, CHUNKS, drain, 0)


def shards(queries, keys, values, block_lists):
    rows, width = queries.shape
    vmem = pl.BlockSpec(memory_space=pltpu.VMEM)
    anywhere = pl.BlockSpec(memory_space=pl.ANY)
    return pl.pallas_call(
        kernel,
        out_shape=jax.ShapeDtypeStruct((rows, width), jnp.bfloat16),
        in_specs=[anywhere, anywhere, anywhere, vmem],
        out_specs=vmem,
        scratch_shapes=[
            pltpu.VMEM((2, CHUNKS, rows, HALF), jnp.bfloat16),
            pltpu.VMEM((BIAS_ROWS, rows), jnp.float32),
            pltpu.VMEM((SLOTS, CHUNKS, rows, 2 * HALF), jnp.bfloat16),
            pltpu.VMEM((2, HEADS, rows, DH), jnp.float32),
            pltpu.VMEM((2, HEADS, rows, DH), jnp.float32),
            pltpu.VMEM((2, HEADS, rows, DH), jnp.float32),
            pltpu.VMEM((CHUNKS, rows, HALF), jnp.bfloat16),
            pltpu.VMEM((CHUNKS, 8, rows), jnp.float32),
            pltpu.VMEM((CHUNKS, rows, HALF), jnp.bfloat16),
            pltpu.VMEM((CHUNKS, 8, rows), jnp.float32),
            pltpu.SemaphoreType.DMA((CHUNKS, 3)),
            pltpu.SemaphoreType.DMA((9, CHUNKS)),
            pltpu.SemaphoreType.DMA((SLOTS, CHUNKS)),
            pltpu.SemaphoreType.DMA((CHUNKS,)),
            pltpu.SemaphoreType.DMA((CHUNKS,)),
            pltpu.SemaphoreType.DMA((CHUNKS,)),
            pltpu.SemaphoreType.DMA((CHUNKS,)),
            pltpu.SemaphoreType.DMA((CHUNKS,)),
            pltpu.SemaphoreType.DMA((CHUNKS,)),
        ],
        compiler_params=pltpu.CompilerParams(
            collective_id=0, has_side_effects=True, vmem_limit_bytes=67043328
        ),
    )(queries, keys, values, block_lists.T)


def solution(mesh):
    placed = P(("tile", "frame"), None)
    return jax.shard_map(
        shards, mesh=mesh, in_specs=(placed, placed, placed, P()), out_specs=placed, check_vma=False
    )
```
